32 devices in a mesh: seq: 4 (over z), head: 8 (over y, x, core).
Axes of the slice: x: 2, y: 2, z: 4, core: 2. Of those that a mesh axis runs over, the one named last changes fastest.
Arguments:
- query: float32 [3072, 1024], P('seq', 'head'), may hold values from -6 to 6
- key_in: float32 [3072, 1024], P('seq', 'head'), may hold values from -6 to 6
- value: float32 [3072, 1024], P('seq', 'head'), may hold values from -6 to 6
- out_grad: float32 [3072, 1024], P('seq', 'head'), may hold values from -6 to 6
- head_scale: float32 [8], P('head'), may hold values from 0.5 to 2
- norm_gain: float32 [1024], P('head'), may hold values from 0.5 to 1.5
- group_counts: int32 [4], replicated, may hold values from 1 to 6, 12 in all
Outputs:
- normed: float32 [3072, 1024], P('seq', 'head')
- grad_query: float32 [3072, 1024], P('seq', 'head')
- grad_key: float32 [3072, 1024], P('seq', 'head')
- grad_value: float32 [3072, 1024], P('seq', 'head')
The draws below stay inside these ranges and needn't reach their ends.
Inputs may be any that keep to these rules, and one draw needn't show every extreme that they name: The live rows of shard i are its first 128 * group_counts[i] rows; the counts sum to 3 * 4 and the largest is exactly 6.
All inputs are finite; a program needn't handle non-finite values.
Results may differ from the reference program's by a relative error of at most 0.0001.
Values sent between devices are 32-bit elements; how exact they have to be, the bound alone decides.
A program may use at most 64 MiB of HBM per device.

```python
import math
import jax
import jax.numpy as jnp
import numpy as np
from jax import lax

DH = 128
HEADS = 8
GROUP = 128
MEAN_GROUPS = 3
CAP = 768
SEQ_BUF = 3072
WIDTH = 1024
N_SEQ = 4


def shard_levels(stream_key, extent, split, low, largest):
    loudness = 1.0
    for dim, parts in split:
        draws = jax.random.uniform(jax.random.fold_in(jax.random.fold_in(stream_key, 6), dim), (parts,), jnp.float32, low / len(split), largest / len(split))
        loudness = loudness * jnp.repeat(jnp.exp(draws), extent[dim] // parts).reshape((-1,) + (1,) * (len(extent) - 1 - dim))
    return loudness


def length_profile(amount, total, most, lean):
    weights = [(1 << 20) // math.isqrt(grade ** lean) + 1 for grade in range(2, amount + 1)]
    rest, holding = total - most - (amount - 1), [1] * (amount - 1)
    while rest > 0:
        free = [i for i in range(amount - 1) if holding[i] < most]
        pool, remaining = sum([weights[i] for i in free]), rest
        for i in free:
            more = min(most - holding[i], max(1, remaining * weights[i] // pool), rest)
            holding[i] = holding[i] + more
            rest = rest - more
    return np.array([most] + holding)


def ragged_sizes(own_key, count, total, most, lean):
    if count == 2:
        one = jax.random.randint(own_key, (), max(1, total - most), min(most, total - 1) + 1)
        return jnp.stack([one, total - one])
    sizes = jnp.asarray(length_profile(count, total, most, lean), jnp.int32)
    couples = (count - 1) // 2
    giver, sink = sizes[1:1 + 2 * couples:2], sizes[2:2 + 2 * couples:2]
    room = jnp.minimum(giver - 1, most - sink)
    passed = jax.random.randint(jax.random.fold_in(own_key, 1), (couples,), 0, 1 << 20) % (room + 1)
    sizes = sizes.at[1:1 + 2 * couples:2].set(giver - passed).at[2:2 + 2 * couples:2].set(sink + passed)
    return sizes[jax.random.permutation(jax.random.fold_in(own_key, 2), count)]


def noise(key, shape, spread, limit, cuts=(), kind=jnp.bfloat16):
    result = spread * jax.random.normal(key, shape, jnp.float32)
    if cuts:
        result = result * shard_levels(key, shape, cuts, -0.22, 0.18)
    return jnp.clip(result, -limit, limit).astype(kind)


def setup_inputs(seed: int = 0) -> dict:
    key_of = jax.random.split(jax.random.key(seed), 8)
    query = noise(key_of[0], (SEQ_BUF, WIDTH), 1.0, 6.0, ((0, 4), (1, 8)), jnp.float32)
    key_in = noise(key_of[1], (SEQ_BUF, WIDTH), 1.0, 6.0, ((0, 4), (1, 8)), jnp.float32)
    value = noise(key_of[2], (SEQ_BUF, WIDTH), 1.0, 6.0, ((0, 4), (1, 8)), jnp.float32)
    out_grad = noise(key_of[3], (SEQ_BUF, WIDTH), 1.0, 6.0, ((0, 4), (1, 8)), jnp.float32)
    head_scale = jnp.clip(jnp.exp(math.log(2.0) - 1.3862944 * jax.random.uniform(key_of[4], (HEADS,), jnp.float32) ** shard_levels(key_of[4], (HEADS,), ((0, 8),), -0.2, 0.2)), 0.5, 2.0)
    norm_gain = jnp.clip(1.0 + 0.1 * jax.random.normal(key_of[5], (WIDTH,), jnp.float32), 0.5, 1.5)
    group_counts = ragged_sizes(key_of[6], N_SEQ, MEAN_GROUPS * N_SEQ, 2 * MEAN_GROUPS, 2).astype(jnp.int32)
    return dict(query=query, key_in=key_in, value=value, out_grad=out_grad, head_scale=head_scale, norm_gain=norm_gain, group_counts=group_counts)


def reference(query, key_in, value, out_grad, head_scale, norm_gain, group_counts):
    row_ids = jnp.arange(SEQ_BUF)
    shard_ids = row_ids // CAP
    live_rows = (row_ids - shard_ids * CAP < group_counts[shard_ids] * GROUP)[:, None]
    causal = jnp.tril(jnp.ones((GROUP, GROUP), dtype=bool))
    highest = lax.Precision.HIGHEST

    def forward_layer(q_all, k_all, v_all):
        blocks = tuple((jnp.where(live_rows, source, 0.0).reshape(SEQ_BUF // GROUP, GROUP, HEADS, DH) for source in (q_all, k_all, v_all)))

        def advance(running, block_items):
            q_block, k_block, v_block = block_items
            scores = jnp.einsum('thd,shd->hts', q_block, k_block, precision=highest)
            scores = jnp.where(causal[None], scores, 0.0)
            local_part = jnp.einsum('hts,shd->thd', scores, v_block, precision=highest)
            carried = jnp.einsum('thd,hde->the', q_block, running, precision=highest)
            running = running + jnp.einsum('shd,she->hde', k_block, v_block, precision=highest)
            return (running, local_part + carried)
        start_state = jnp.zeros((HEADS, DH, DH), jnp.float32)
        _, attended = lax.scan(advance, start_state, blocks)
        attended = attended.reshape(SEQ_BUF, HEADS, DH) * head_scale[None, :, None]
        scaled = attended.reshape(SEQ_BUF, WIDTH)
        inverse = lax.rsqrt(lax.optimization_barrier(jnp.mean(scaled * scaled, axis=1, keepdims=True)) + 1e-05)
        return scaled * inverse * norm_gain[None, :]
    normed, pullback = jax.vjp(forward_layer, query, key_in, value)
    grad_query, grad_key, grad_value = pullback(out_grad)
    return (normed, grad_query, grad_key, grad_value)
```

```python
import functools

import jax
import jax.numpy as jnp
from jax import lax
from jax.experimental import pallas as pl
from jax.experimental.pallas import tpu as pltpu
from jax.sharding import PartitionSpec as P

GROUP = 128
CHUNKS = 4
EPS = 1e-05
F32 = jnp.float32
BF16 = jnp.bfloat16
NN = (((1,), (0,)), ((), ()))
NT = (((1,), (1,)), ((), ()))
TN = (((0,), (0,)), ((), ()))


def dot(left, right, dims):
    return lax.dot_general(left, right, dims, preferred_element_type=F32)


def split(x):
    high = x.astype(BF16)
    low = (x - high.astype(F32)).astype(BF16)
    return high, low


def rows_by_rows(a, b):
    left = jnp.concatenate([a[0], a[1], a[0]], axis=1)
    right = jnp.concatenate([b[0], b[0], b[1]], axis=1)
    return dot(left, right, NT)


def times(a, b):
    d = b[0].shape[1]
    both = dot(a[0], jnp.concatenate([b[0], b[1]], axis=1), NN)
    return both[:, :d] + both[:, d:] + dot(a[1], b[0], NN)


def times_state(a, s):
    d = s[0].shape[1]
    left = jnp.concatenate([a[0], a[1]], axis=1)
    top = jnp.concatenate([s[0], s[1]], axis=1)
    bottom = jnp.concatenate([s[0], jnp.zeros_like(s[0])], axis=1)
    both = dot(left, jnp.concatenate([top, bottom], axis=0), NN)
    return both[:, :d] + both[:, d:]


def times_state_t(a, s):
    d = s[0].shape[0]
    left = jnp.concatenate([a[0], a[1]], axis=1)
    top = jnp.concatenate([s[0], s[0]], axis=1)
    bottom = jnp.concatenate([s[1], jnp.zeros_like(s[1])], axis=1)
    both = dot(left, jnp.concatenate([top, bottom], axis=0), NT)
    return both[:, :d] + both[:, d:]


def outer(a, b):
    d = a[0].shape[1]
    full = dot(jnp.concatenate(a, axis=1), jnp.concatenate(b, axis=1), TN)
    return full[:d, :d] + full[:d, d:] + full[d:, :d] + full[d:, d:]


def row_sums(x):
    high, low = split(x)
    low2 = (x - high.astype(F32) - low.astype(F32)).astype(BF16)
    parts = jnp.concatenate([high, low, low2], axis=1)
    return dot(jnp.ones((8, parts.shape[1]), BF16), parts, NT)[0:1]


def kernel(
    n_seq, n_head, block, counts, head_scale,
    q_hbm, k_hbm, v_hbm, g_hbm, gain_hbm,
    normed_hbm, gq_hbm, gk_hbm, gv_hbm,
    q_in, k_in, v_in, g_in, gain,
    q_h, q_l, k_h, k_l, v_h, v_l, o_h, o_l, p_h, p_l,
    scaled, normed, gq, gk, gv,
    send_s, recv_s, send_t, recv_t, sums, sums_in,
    in_sem, out_sem, s_send, s_recv, t_send, t_recv, h_send, h_recv,
):
    cap, d = q_in.shape
    blocks = cap // block
    per = block // GROUP
    pos = lax.axis_index("seq")
    head = lax.axis_index("head")
    half = sums.shape[0] // 2

    loads = [
        pltpu.make_async_copy(src, dst, in_sem.at[i])
        for i, (src, dst) in enumerate(
            ((k_hbm, k_in), (v_hbm, v_in), (q_hbm, q_in), (g_hbm, g_in), (gain_hbm, gain))
        )
    ]
    for load in loads:
        load.start()

    first, last = pos == 0, pos == n_seq - 1
    barrier = pltpu.get_barrier_semaphore()

    @pl.when(jnp.logical_not(first))
    def _():
        pl.semaphore_signal(barrier, inc=1, device_id={"seq": pos - 1}, device_id_type=pl.DeviceIdType.MESH)

    @pl.when(jnp.logical_not(last))
    def _():
        pl.semaphore_signal(barrier, inc=1, device_id={"seq": pos + 1}, device_id_type=pl.DeviceIdType.MESH)

    for step in range(1, n_head):
        pl.semaphore_signal(
            barrier, inc=1, device_id={"head": lax.rem(head + step, n_head)},
            device_id_type=pl.DeviceIdType.MESH,
        )

    live = counts[pos] * GROUP
    row = lax.broadcasted_iota(jnp.int32, (block, d), 0)
    t_row = lax.broadcasted_iota(jnp.int32, (block, block), 0)
    t_col = lax.broadcasted_iota(jnp.int32, (block, block), 1)

    def take(b):
        return pl.ds(b * block, block)

    def pair(high, low, b):
        return high[take(b), :], low[take(b), :]

    def keep(source, high, low, b):
        x = jnp.where(row + b * block < live, source[take(b), :], 0.0)
        high[take(b), :], low[take(b), :] = split(x)

    sums[...] = jnp.zeros_like(sums)
    loads[0].wait()
    loads[1].wait()
    states = []
    for b in range(blocks):
        keep(k_in, k_h, k_l, b)
        keep(v_in, v_h, v_l, b)
        states.append(outer(pair(k_h, k_l, b), pair(v_h, v_l, b)))
    before = [jnp.zeros((d, d), F32)]
    for b in range(blocks):
        before.append(before[-1] + states[b])

    def piece(c):
        return pl.ds(c * (d // CHUNKS), d // CHUNKS)

    def hop(src, dst, s_sem, r_sem, c, target):
        return pltpu.make_async_remote_copy(
            src_ref=src.at[piece(c), :], dst_ref=dst.at[piece(c), :],
            send_sem=s_sem.at[c], recv_sem=r_sem.at[c],
            device_id={"seq": target}, device_id_type=pl.DeviceIdType.MESH,
        )

    send_s[...] = before[-1]
    pl.semaphore_wait(
        barrier,
        n_head - 1 + jnp.where(first, 0, 1) + jnp.where(last, 0, 1),
    )

    @pl.when(first)
    def _():
        for c in range(CHUNKS):
            hop(send_s, recv_s, s_send, s_recv, c, pos + 1).start()
        recv_s[...] = jnp.zeros_like(recv_s)

    loads[2].wait()
    for b in range(blocks):
        keep(q_in, q_h, q_l, b)
        q_b, k_b = pair(q_h, q_l, b), pair(k_h, k_l, b)
        scores = jnp.where(t_row >= t_col, rows_by_rows(q_b, k_b), 0.0)
        scaled[take(b), :] = times(split(scores), pair(v_h, v_l, b))

    @pl.when(jnp.logical_not(first))
    def _():
        for c in range(CHUNKS):
            hop(send_s, recv_s, s_send, s_recv, c, pos).wait_recv()

            @pl.when(jnp.logical_not(last))
            def _():
                send_s[piece(c), :] += recv_s[piece(c), :]
                hop(send_s, recv_s, s_send, s_recv, c, pos + 1).start()

    loads[3].wait()
    loads[4].wait()
    scale = head_scale[0]
    gains = gain[...].reshape(1, d)
    for b in range(blocks):
        state = recv_s[...] + before[b]
        mine = (scaled[take(b), :] + times_state(pair(q_h, q_l, b), split(state))) * scale
        scaled[take(b), :] = mine
        square = row_sums(mine * mine)
        cross = row_sums(gains * g_in[take(b), :] * mine)
        for j in range(per):
            sums[b * per + j : b * per + j + 1, :] = square[:, j * GROUP : (j + 1) * GROUP]
            sums[half + b * per + j : half + b * per + j + 1, :] = cross[:, j * GROUP : (j + 1) * GROUP]

    shares = [
        pltpu.make_async_remote_copy(
            src_ref=sums, dst_ref=sums_in.at[step - 1],
            send_sem=h_send.at[step - 1], recv_sem=h_recv.at[step - 1],
            device_id={"head": lax.rem(head + step, n_head)},
            device_id_type=pl.DeviceIdType.MESH,
        )
        for step in range(1, n_head)
    ]
    for share in shares:
        share.start()

    for b in range(blocks):
        q_b, k_b = pair(q_h, q_l, b), pair(k_h, k_l, b)
        scores_t = jnp.where(t_row <= t_col, rows_by_rows(k_b, q_b), 0.0)
        p_h[take(b), :], p_l[take(b), :] = split(scores_t)

    total = sums[...]
    for step in range(1, n_head):
        shares[step - 1].wait_recv()
        total = total + sums_in[step - 1]
    features = d * n_head
    inverse = lax.rsqrt(total[:half] / features + EPS)
    factor = inverse * inverse * inverse * total[half:] / features
    columns = jnp.transpose(jnp.concatenate([inverse, factor], axis=0))

    t_states = []
    for b in range(blocks):
        inv = jnp.concatenate(
            [jnp.broadcast_to(columns[:, b * per + j : b * per + j + 1], (GROUP, d)) for j in range(per)], axis=0
        )
        fac = jnp.concatenate(
            [jnp.broadcast_to(columns[:, half + b * per + j : half + b * per + j + 1], (GROUP, d)) for j in range(per)],
            axis=0,
        )
        mine = scaled[take(b), :]
        weight = inv * gains
        normed[take(b), :] = mine * weight
        grad = (weight * g_in[take(b), :] - mine * fac) * scale
        grad = jnp.where(row + b * block < live, grad, 0.0)
        o_h[take(b), :], o_l[take(b), :] = split(grad)
        t_states.append(outer(pair(q_h, q_l, b), pair(o_h, o_l, b)))
    after = [jnp.zeros((d, d), F32)]
    for b in range(blocks - 1, -1, -1):
        after.append(after[-1] + t_states[b])
    after = after[::-1]

    send_t[...] = after[0]

    @pl.when(last)
    def _():
        for c in range(CHUNKS):
            hop(send_t, recv_t, t_send, t_recv, c, pos - 1).start()
        recv_t[...] = jnp.zeros_like(recv_t)

    store_normed = pltpu.make_async_copy(normed, normed_hbm, out_sem.at[0])
    store_normed.start()
    for b in range(blocks):
        o_b, v_b = pair(o_h, o_l, b), pair(v_h, v_l, b)
        pulled = jnp.where(t_row >= t_col, rows_by_rows(o_b, v_b), 0.0)
        pulled_t = jnp.where(t_row <= t_col, rows_by_rows(v_b, o_b), 0.0)
        state = recv_s[...] + before[b]
        gq[take(b), :] = times_state_t(o_b, split(state)) + times(split(pulled), pair(k_h, k_l, b))
        gk[take(b), :] = times(split(pulled_t), pair(q_h, q_l, b))
        gv[take(b), :] = times(pair(p_h, p_l, b), o_b)
    store_gq = pltpu.make_async_copy(gq, gq_hbm, out_sem.at[1])
    store_gq.start()

    @pl.when(jnp.logical_not(last))
    def _():
        for c in range(CHUNKS):
            hop(send_t, recv_t, t_send, t_recv, c, pos).wait_recv()

            @pl.when(jnp.logical_not(first))
            def _():
                send_t[piece(c), :] += recv_t[piece(c), :]
                hop(send_t, recv_t, t_send, t_recv, c, pos - 1).start()

    for b in range(blocks):
        state = split(recv_t[...] + after[b + 1])
        gk[take(b), :] += times_state_t(pair(v_h, v_l, b), state)
        gv[take(b), :] += times_state(pair(k_h, k_l, b), state)
    store_gk = pltpu.make_async_copy(gk, gk_hbm, out_sem.at[2])
    store_gv = pltpu.make_async_copy(gv, gv_hbm, out_sem.at[3])
    store_gk.start()
    store_gv.start()

    for share in shares:
        share.wait_send()

    @pl.when(jnp.logical_not(last))
    def _():
        for c in range(CHUNKS):
            hop(send_s, recv_s, s_send, s_recv, c, pos + 1).wait_send()

    @pl.when(jnp.logical_not(first))
    def _():
        for c in range(CHUNKS):
            hop(send_t, recv_t, t_send, t_recv, c, pos - 1).wait_send()

    store_normed.wait()
    store_gq.wait()
    store_gk.wait()
    store_gv.wait()


def on_device(n_seq, n_head, query, key_in, value, out_grad, head_scale, norm_gain, group_counts):
    cap, d = query.shape
    block = 2 * GROUP if cap % (2 * GROUP) == 0 else GROUP
    half = -(-(cap // GROUP) // 8) * 8
    any_space = pl.BlockSpec(memory_space=pl.ANY)
    smem = pl.BlockSpec(memory_space=pltpu.SMEM)
    wide = pltpu.VMEM((cap, d), F32)
    narrow = pltpu.VMEM((cap, d), BF16)
    state = pltpu.VMEM((d, d), F32)
    return pl.pallas_call(
        functools.partial(kernel, n_seq, n_head, block),
        out_shape=[jax.ShapeDtypeStruct((cap, d), F32)] * 4,
        in_specs=[smem, smem] + [any_space] * 5,
        out_specs=[any_space] * 4,
        scratch_shapes=[wide] * 4 + [pltpu.VMEM((d,), F32)]
        + [narrow] * 8 + [pltpu.VMEM((cap, block), BF16)] * 2
        + [wide] * 5
        + [state] * 4
        + [pltpu.VMEM((2 * half, GROUP), F32), pltpu.VMEM((n_head - 1, 2 * half, GROUP), F32)]
        + [pltpu.SemaphoreType.DMA((5,)), pltpu.SemaphoreType.DMA((4,))]
        + [pltpu.SemaphoreType.DMA((CHUNKS,))] * 4
        + [pltpu.SemaphoreType.DMA((n_head - 1,))] * 2,
        compiler_params=pltpu.CompilerParams(
            collective_id=0, has_side_effects=True, vmem_limit_bytes=48 * 1024 * 1024
        ),
    )(group_counts, head_scale, query, key_in, value, out_grad, norm_gain)


def solution(mesh):
    rows = P("seq", "head")
    return jax.shard_map(
        functools.partial(on_device, mesh.shape["seq"], mesh.shape["head"]),
        mesh=mesh,
        in_specs=(rows, rows, rows, rows, P("head"), P("head"), P()),
        out_specs=(rows, rows, rows, rows),
        check_vma=False,
    )
```

```python
import functools

import jax
import jax.numpy as jnp
from jax import lax
from jax.experimental import pallas as pl
from jax.experimental.pallas import tpu as pltpu
from jax.sharding import PartitionSpec as P

GROUP = 128
CHUNKS = 4
EPS = 1e-05
F32 = jnp.float32
BF16 = jnp.bfloat16
NN = (((1,), (0,)), ((), ()))
NT = (((1,), (1,)), ((), ()))
TN = (((0,), (0,)), ((), ()))


def dot(left, right, dims):
    return lax.dot_general(left, right, dims, preferred_element_type=F32)


def split(x):
    high = x.astype(BF16)
    low = (x - high.astype(F32)).astype(BF16)
    return high, low


def rows_by_rows(a, b):
    left = jnp.concatenate([a[0], a[1], a[0]], axis=1)
    right = jnp.concatenate([b[0], b[0], b[1]], axis=1)
    return dot(left, right, NT)


def times(a, b):
    d = b[0].shape[1]
    both = dot(a[0], jnp.concatenate([b[0], b[1]], axis=1), NN)
    return both[:, :d] + both[:, d:] + dot(a[1], b[0], NN)


def times_state(a, s):
    d = s[0].shape[1]
    left = jnp.concatenate([a[0], a[1]], axis=1)
    top = jnp.concatenate([s[0], s[1]], axis=1)
    bottom = jnp.concatenate([s[0], jnp.zeros_like(s[0])], axis=1)
    both = dot(left, jnp.concatenate([top, bottom], axis=0), NN)
    return both[:, :d] + both[:, d:]


def times_state_t(a, s):
    d = s[0].shape[0]
    left = jnp.concatenate([a[0], a[1]], axis=1)
    top = jnp.concatenate([s[0], s[0]], axis=1)
    bottom = jnp.concatenate([s[1], jnp.zeros_like(s[1])], axis=1)
    both = dot(left, jnp.concatenate([top, bottom], axis=0), NT)
    return both[:, :d] + both[:, d:]


def outer(a, b):
    d = a[0].shape[1]
    full = dot(jnp.concatenate(a, axis=1), jnp.concatenate(b, axis=1), TN)
    return full[:d, :d] + full[:d, d:] + full[d:, :d] + full[d:, d:]


def row_sums(x):
    high, low = split(x)
    low2 = (x - high.astype(F32) - low.astype(F32)).astype(BF16)
    parts = jnp.concatenate([high, low, low2], axis=1)
    return dot(jnp.ones((8, parts.shape[1]), BF16), parts, NT)[0:1]


def kernel(
    n_seq, n_head, block, head_scale, counts_hbm,
    q_hbm, k_hbm, v_hbm, g_hbm, gain_hbm,
    normed, gq, gk, gv, k_h, k_l, v_h, v_l, t_out,
    counts, q_in, k_in, v_in, g_in, gain,
    q_h, q_l, o_h, o_l, p_h, p_l,
    scaled, send_s, recv_s, send_t, recv_t, sums, sums_in,
    in_sem, s_send, s_recv, t_send, t_recv, h_send, h_recv,
):
    cap, d = q_in.shape
    blocks = cap // block
    per = block // GROUP
    pos = lax.axis_index("seq")
    head = lax.axis_index("head")
    half = sums.shape[0] // 2

    loads = [
        pltpu.make_async_copy(src, dst, in_sem.at[i])
        for i, (src, dst) in enumerate(
            (
                (counts_hbm, counts), (k_hbm, k_in), (v_hbm, v_in), (q_hbm, q_in),
                (g_hbm, g_in), (gain_hbm, gain),
            )
        )
    ]
    for load in loads:
        load.start()

    first, last = pos == 0, pos == n_seq - 1
    barrier = pltpu.get_barrier_semaphore()

    @pl.when(jnp.logical_not(first))
    def _():
        pl.semaphore_signal(barrier, inc=1, device_id={"seq": pos - 1}, device_id_type=pl.DeviceIdType.MESH)

    @pl.when(jnp.logical_not(last))
    def _():
        pl.semaphore_signal(barrier, inc=1, device_id={"seq": pos + 1}, device_id_type=pl.DeviceIdType.MESH)

    for step in range(1, n_head):
        pl.semaphore_signal(
            barrier, inc=1, device_id={"head": lax.rem(head + step, n_head)},
            device_id_type=pl.DeviceIdType.MESH,
        )

    loads[0].wait()
    live = counts[pos] * GROUP
    row = lax.broadcasted_iota(jnp.int32, (block, d), 0)
    t_row = lax.broadcasted_iota(jnp.int32, (block, block), 0)
    t_col = lax.broadcasted_iota(jnp.int32, (block, block), 1)

    def take(b):
        return pl.ds(b * block, block)

    def pair(high, low, b):
        return high[take(b), :], low[take(b), :]

    def keep(source, high, low, b):
        x = jnp.where(row + b * block < live, source[take(b), :], 0.0)
        high[take(b), :], low[take(b), :] = split(x)

    sums[...] = jnp.zeros_like(sums)
    loads[1].wait()
    loads[2].wait()
    states = []
    for b in range(blocks):
        keep(k_in, k_h, k_l, b)
        keep(v_in, v_h, v_l, b)
        states.append(outer(pair(k_h, k_l, b), pair(v_h, v_l, b)))
    before = [jnp.zeros((d, d), F32)]
    for b in range(blocks):
        before.append(before[-1] + states[b])

    def piece(c):
        return pl.ds(c * (d // CHUNKS), d // CHUNKS)

    def hop(src, dst, s_sem, r_sem, c, target):
        return pltpu.make_async_remote_copy(
            src_ref=src.at[piece(c), :], dst_ref=dst.at[piece(c), :],
            send_sem=s_sem.at[c], recv_sem=r_sem.at[c],
            device_id={"seq": target}, device_id_type=pl.DeviceIdType.MESH,
        )

    send_s[...] = before[-1]
    pl.semaphore_wait(
        barrier,
        n_head - 1 + jnp.where(first, 0, 1) + jnp.where(last, 0, 1),
    )

    @pl.when(first)
    def _():
        for c in range(CHUNKS):
            hop(send_s, recv_s, s_send, s_recv, c, pos + 1).start()
        recv_s[...] = jnp.zeros_like(recv_s)

    loads[3].wait()
    for b in range(blocks):
        keep(q_in, q_h, q_l, b)
        q_b, k_b = pair(q_h, q_l, b), pair(k_h, k_l, b)
        scores = jnp.where(t_row >= t_col, rows_by_rows(q_b, k_b), 0.0)
        scaled[take(b), :] = times(split(scores), pair(v_h, v_l, b))

    @pl.when(jnp.logical_not(first))
    def _():
        for c in range(CHUNKS):
            hop(send_s, recv_s, s_send, s_recv, c, pos).wait_recv()

            @pl.when(jnp.logical_not(last))
            def _():
                send_s[piece(c), :] += recv_s[piece(c), :]
                hop(send_s, recv_s, s_send, s_recv, c, pos + 1).start()

    loads[4].wait()
    loads[5].wait()
    scale = head_scale[0]
    gains = gain[...].reshape(1, d)
    for b in range(blocks):
        state = recv_s[...] + before[b]
        mine = (scaled[take(b), :] + times_state(pair(q_h, q_l, b), split(state))) * scale
        scaled[take(b), :] = mine
        square = row_sums(mine * mine)
        cross = row_sums(gains * g_in[take(b), :] * mine)
        for j in range(per):
            sums[b * per + j : b * per + j + 1, :] = square[:, j * GROUP : (j + 1) * GROUP]
            sums[half + b * per + j : half + b * per + j + 1, :] = cross[:, j * GROUP : (j + 1) * GROUP]

    shares = [
        pltpu.make_async_remote_copy(
            src_ref=sums, dst_ref=sums_in.at[step - 1],
            send_sem=h_send.at[step - 1], recv_sem=h_recv.at[step - 1],
            device_id={"head": lax.rem(head + step, n_head)},
            device_id_type=pl.DeviceIdType.MESH,
        )
        for step in range(1, n_head)
    ]
    for share in shares:
        share.start()

    for b in range(blocks):
        q_b, k_b = pair(q_h, q_l, b), pair(k_h, k_l, b)
        scores_t = jnp.where(t_row <= t_col, rows_by_rows(k_b, q_b), 0.0)
        p_h[take(b), :], p_l[take(b), :] = split(scores_t)

    total = sums[...]
    for step in range(1, n_head):
        shares[step - 1].wait_recv()
        total = total + sums_in[step - 1]
    features = d * n_head
    inverse = lax.rsqrt(total[:half] / features + EPS)
    factor = inverse * inverse * inverse * total[half:] / features
    columns = jnp.transpose(jnp.concatenate([inverse, factor], axis=0))

    t_states = []
    for b in range(blocks):
        inv = jnp.concatenate(
            [jnp.broadcast_to(columns[:, b * per + j : b * per + j + 1], (GROUP, d)) for j in range(per)], axis=0
        )
        fac = jnp.concatenate(
            [jnp.broadcast_to(columns[:, half + b * per + j : half + b * per + j + 1], (GROUP, d)) for j in range(per)],
            axis=0,
        )
        mine = scaled[take(b), :]
        weight = inv * gains
        normed[take(b), :] = mine * weight
        grad = (weight * g_in[take(b), :] - mine * fac) * scale
        grad = jnp.where(row + b * block < live, grad, 0.0)
        o_h[take(b), :], o_l[take(b), :] = split(grad)
        t_states.append(outer(pair(q_h, q_l, b), pair(o_h, o_l, b)))
    after = [jnp.zeros((d, d), F32)]
    for b in range(blocks - 1, -1, -1):
        after.append(after[-1] + t_states[b])
    after = after[::-1]

    send_t[...] = after[0]

    @pl.when(last)
    def _():
        for c in range(CHUNKS):
            hop(send_t, recv_t, t_send, t_recv, c, pos - 1).start()
        recv_t[...] = jnp.zeros_like(recv_t)

    for b in range(blocks):
        o_b, v_b = pair(o_h, o_l, b), pair(v_h, v_l, b)
        pulled = jnp.where(t_row >= t_col, rows_by_rows(o_b, v_b), 0.0)
        pulled_t = jnp.where(t_row <= t_col, rows_by_rows(v_b, o_b), 0.0)
        state = recv_s[...] + before[b]
        gq[take(b), :] = times_state_t(o_b, split(state)) + times(split(pulled), pair(k_h, k_l, b))
        gk[take(b), :] = times(split(pulled_t), pair(q_h, q_l, b))
        gv[take(b), :] = times(pair(p_h, p_l, b), o_b)

    @pl.when(jnp.logical_not(last))
    def _():
        for c in range(CHUNKS):
            hop(send_t, recv_t, t_send, t_recv, c, pos).wait_recv()

            @pl.when(jnp.logical_not(first))
            def _():
                send_t[piece(c), :] += recv_t[piece(c), :]
                hop(send_t, recv_t, t_send, t_recv, c, pos - 1).start()

    for b in range(blocks):
        t_out[b] = recv_t[...] + after[b + 1]

    for share in shares:
        share.wait_send()

    @pl.when(jnp.logical_not(last))
    def _():
        for c in range(CHUNKS):
            hop(send_s, recv_s, s_send, s_recv, c, pos + 1).wait_send()

    @pl.when(jnp.logical_not(first))
    def _():
        for c in range(CHUNKS):
            hop(send_t, recv_t, t_send, t_recv, c, pos - 1).wait_send()


def finish(
    block, normed, gq, gk, gv, k_h, k_l, v_h, v_l, t_in,
    normed_hbm, gq_hbm, gk_hbm, gv_hbm, gk_all, gv_all, sem,
):
    blocks = t_in.shape[0]
    stores = [
        pltpu.make_async_copy(normed, normed_hbm, sem.at[2 * blocks]),
        pltpu.make_async_copy(gq, gq_hbm, sem.at[2 * blocks + 1]),
    ]
    for store in stores:
        store.start()
    for b in range(blocks):
        rows = pl.ds(b * block, block)
        state = split(t_in[b])
        gk_all[rows, :] = gk[rows, :] + times_state_t((v_h[rows, :], v_l[rows, :]), state)
        gv_all[rows, :] = gv[rows, :] + times_state((k_h[rows, :], k_l[rows, :]), state)
        for i, (src, dst) in enumerate(((gk_all, gk_hbm), (gv_all, gv_hbm))):
            store = pltpu.make_async_copy(src.at[rows, :], dst.at[rows, :], sem.at[2 * b + i])
            store.start()
            stores.append(store)
    for store in stores:
        store.wait()


def on_device(n_seq, n_head, query, key_in, value, out_grad, head_scale, norm_gain, group_counts):
    cap, d = query.shape
    block = 2 * GROUP if cap % (2 * GROUP) == 0 else GROUP
    half = -(-(cap // GROUP) // 8) * 8
    blocks = cap // block
    hbm = pl.BlockSpec(memory_space=pltpu.HBM)
    vmem = pl.BlockSpec(memory_space=pltpu.VMEM)
    wide = pltpu.VMEM((cap, d), F32)
    narrow = pltpu.VMEM((cap, d), BF16)
    state = pltpu.VMEM((d, d), F32)
    rows = jax.ShapeDtypeStruct((cap, d), F32)
    rows_low = jax.ShapeDtypeStruct((cap, d), BF16)
    held = pl.pallas_call(
        functools.partial(kernel, n_seq, n_head, block),
        out_shape=[rows] * 4 + [rows_low] * 4 + [jax.ShapeDtypeStruct((blocks, d, d), F32)],
        in_specs=[pl.BlockSpec(memory_space=pltpu.SMEM)] + [hbm] * 6,
        out_specs=[vmem] * 9,
        scratch_shapes=[pltpu.SMEM(group_counts.shape, jnp.int32)]
        + [wide] * 4 + [pltpu.VMEM((d,), F32)]
        + [narrow] * 4 + [pltpu.VMEM((cap, block), BF16)] * 2
        + [wide]
        + [state] * 4
        + [pltpu.VMEM((2 * half, GROUP), F32), pltpu.VMEM((n_head - 1, 2 * half, GROUP), F32)]
        + [pltpu.SemaphoreType.DMA((6,))]
        + [pltpu.SemaphoreType.DMA((CHUNKS,))] * 4
        + [pltpu.SemaphoreType.DMA((n_head - 1,))] * 2,
        compiler_params=pltpu.CompilerParams(
            collective_id=0, has_side_effects=True, vmem_limit_bytes=32 * 1024 * 1024
        ),
    )(head_scale, *(
        pltpu.with_memory_space_constraint(x, pltpu.HBM)
        for x in (group_counts, query, key_in, value, out_grad, norm_gain)
    ))
    return pl.pallas_call(
        functools.partial(finish, block),
        out_shape=[rows] * 4,
        in_specs=[vmem] * 9,
        out_specs=[hbm] * 4,
        scratch_shapes=[wide] * 2 + [pltpu.SemaphoreType.DMA((2 * blocks + 2,))],
        compiler_params=pltpu.CompilerParams(vmem_limit_bytes=32 * 1024 * 1024),
    )(*held)


def solution(mesh):
    rows = P("seq", "head")
    return jax.shard_map(
        functools.partial(on_device, mesh.shape["seq"], mesh.shape["head"]),
        mesh=mesh,
        in_specs=(rows, rows, rows, rows, P("head"), P("head"), P()),
        out_specs=(rows, rows, rows, rows),
        check_vma=False,
    )
```

```python
import functools

import jax
import jax.numpy as jnp
from jax import lax
from jax.experimental import pallas as pl
from jax.experimental.pallas import tpu as pltpu
from jax.sharding import PartitionSpec as P

GROUP = 128
CHUNKS = 4
EPS = 1e-05
F32 = jnp.float32
BF16 = jnp.bfloat16
NN = (((1,), (0,)), ((), ()))
NT = (((1,), (1,)), ((), ()))
TN = (((0,), (0,)), ((), ()))


def dot(left, right, dims):
    return lax.dot_general(left, right, dims, preferred_element_type=F32)


def split(x):
    high = x.astype(BF16)
    low = (x - high.astype(F32)).astype(BF16)
    return high, low


def rows_by_rows(a, b):
    left = jnp.concatenate([a[0], a[1], a[0]], axis=1)
    right = jnp.concatenate([b[0], b[0], b[1]], axis=1)
    return dot(left, right, NT)


def times(a, b):
    d = b[0].shape[1]
    both = dot(a[0], jnp.concatenate([b[0], b[1]], axis=1), NN)
    return both[:, :d] + both[:, d:] + dot(a[1], b[0], NN)


def times_state(a, s):
    d = s[0].shape[1]
    left = jnp.concatenate([a[0], a[1]], axis=1)
    top = jnp.concatenate([s[0], s[1]], axis=1)
    bottom = jnp.concatenate([s[0], jnp.zeros_like(s[0])], axis=1)
    both = dot(left, jnp.concatenate([top, bottom], axis=0), NN)
    return both[:, :d] + both[:, d:]


def times_state_t(a, s):
    d = s[0].shape[0]
    left = jnp.concatenate([a[0], a[1]], axis=1)
    top = jnp.concatenate([s[0], s[0]], axis=1)
    bottom = jnp.concatenate([s[1], jnp.zeros_like(s[1])], axis=1)
    both = dot(left, jnp.concatenate([top, bottom], axis=0), NT)
    return both[:, :d] + both[:, d:]


def outer(a, b):
    d = a[0].shape[1]
    full = dot(jnp.concatenate(a, axis=1), jnp.concatenate(b, axis=1), TN)
    return full[:d, :d] + full[:d, d:] + full[d:, :d] + full[d:, d:]


def row_sums(x):
    high, low = split(x)
    low2 = (x - high.astype(F32) - low.astype(F32)).astype(BF16)
    parts = jnp.concatenate([high, low, low2], axis=1)
    return dot(jnp.ones((8, parts.shape[1]), BF16), parts, NT)[0:1]


def kernel(
    n_seq, n_head, block, head_scale, counts_hbm,
    q_hbm, k_hbm, v_hbm, g_hbm, gain_hbm,
    normed, gq, gk, gv, k_h, k_l, v_h, v_l, t_out,
    counts, q_in, k_in, v_in, g_in, gain,
    q_h, q_l, o_h, o_l, p_h, p_l,
    scaled, send_s, recv_s, send_t, recv_t, end_s, end_t, sums, sums_in,
    in_sem, s_send, s_recv, t_send, t_recv, h_send, h_recv, e_send, e_recv,
):
    cap, d = q_in.shape
    blocks = cap // block
    per = block // GROUP
    pos = lax.axis_index("seq")
    head = lax.axis_index("head")
    half = sums.shape[0] // 2

    loads = [
        pltpu.make_async_copy(src, dst, in_sem.at[i])
        for i, (src, dst) in enumerate(
            (
                (counts_hbm, counts), (k_hbm, k_in), (v_hbm, v_in), (q_hbm, q_in),
                (g_hbm, g_in), (gain_hbm, gain),
            )
        )
    ]
    for load in loads:
        load.start()

    first, last = pos == 0, pos == n_seq - 1
    barrier = pltpu.get_barrier_semaphore()

    direct = 2 < n_seq <= 4

    def greet(other):
        pl.semaphore_signal(barrier, inc=1, device_id={"seq": other}, device_id_type=pl.DeviceIdType.MESH)

    if direct:
        for step in range(1, n_seq):
            greet(lax.rem(pos + step, n_seq))
        seq_peers = n_seq - 1
    else:

        @pl.when(jnp.logical_not(first))
        def _():
            greet(pos - 1)

        @pl.when(jnp.logical_not(last))
        def _():
            greet(pos + 1)

        seq_peers = jnp.where(first, 0, 1) + jnp.where(last, 0, 1)

    for step in range(1, n_head):
        pl.semaphore_signal(
            barrier, inc=1, device_id={"head": lax.rem(head + step, n_head)},
            device_id_type=pl.DeviceIdType.MESH,
        )

    loads[0].wait()
    live = counts[pos] * GROUP
    row = lax.broadcasted_iota(jnp.int32, (block, d), 0)
    t_row = lax.broadcasted_iota(jnp.int32, (block, block), 0)
    t_col = lax.broadcasted_iota(jnp.int32, (block, block), 1)

    def take(b):
        return pl.ds(b * block, block)

    def pair(high, low, b):
        return high[take(b), :], low[take(b), :]

    def keep(source, high, low, b):
        x = jnp.where(row + b * block < live, source[take(b), :], 0.0)
        high[take(b), :], low[take(b), :] = split(x)

    sums[...] = jnp.zeros_like(sums)
    loads[1].wait()
    loads[2].wait()
    states = []
    for b in range(blocks):
        keep(k_in, k_h, k_l, b)
        keep(v_in, v_h, v_l, b)
        states.append(outer(pair(k_h, k_l, b), pair(v_h, v_l, b)))
    before = [jnp.zeros((d, d), F32)]
    for b in range(blocks):
        before.append(before[-1] + states[b])

    def piece(c):
        return pl.ds(c * (d // CHUNKS), d // CHUNKS)

    def hop(src, dst, s_sem, r_sem, c, target):
        return pltpu.make_async_remote_copy(
            src_ref=src.at[piece(c), :], dst_ref=dst.at[piece(c), :],
            send_sem=s_sem.at[c], recv_sem=r_sem.at[c],
            device_id={"seq": target}, device_id_type=pl.DeviceIdType.MESH,
        )

    def reach(src, dst, way, target, step):
        return pltpu.make_async_remote_copy(
            src_ref=src, dst_ref=dst, send_sem=e_send.at[way, step], recv_sem=e_recv.at[way],
            device_id={"seq": target}, device_id_type=pl.DeviceIdType.MESH,
        )

    def exchange(way, src, dst, end, s_sem, r_sem):
        delta = 1 if way == 0 else -1
        order = pos if way == 0 else n_seq - 1 - pos
        head_of_chain = 1 if direct else 0

        def begin():
            if direct:

                @pl.when(order == 0)
                def _():
                    for step in range(n_seq - 1, 0, -1):
                        reach(src, end, way, pos + delta * step, step).start()
                    end[...] = jnp.zeros_like(end)

            @pl.when(order == head_of_chain)
            def _():
                for c in range(CHUNKS):
                    hop(src, dst, s_sem, r_sem, c, pos + delta).start()

            @pl.when(order <= head_of_chain)
            def _():
                dst[...] = jnp.zeros_like(dst)

        def relay():
            @pl.when(order > head_of_chain)
            def _():
                for c in range(CHUNKS):
                    hop(src, dst, s_sem, r_sem, c, pos).wait_recv()

                    @pl.when(order < n_seq - 1)
                    def _():
                        src[piece(c), :] += dst[piece(c), :]
                        hop(src, dst, s_sem, r_sem, c, pos + delta).start()

        def arrive():
            if direct:

                @pl.when(order > 0)
                def _():
                    reach(src, end, way, pos, 0).wait_recv()
                    dst[...] += end[...]

        def close():
            if direct:

                @pl.when(order == 0)
                def _():
                    for step in range(n_seq - 1, 0, -1):
                        reach(src, end, way, pos + delta * step, step).wait_send()

            @pl.when(jnp.logical_and(order >= head_of_chain, order < n_seq - 1))
            def _():
                for c in range(CHUNKS):
                    hop(src, dst, s_sem, r_sem, c, pos + delta).wait_send()

        return begin, relay, arrive, close

    s_begin, s_relay, s_arrive, s_close = exchange(0, send_s, recv_s, end_s, s_send, s_recv)
    t_begin, t_relay, t_arrive, t_close = exchange(1, send_t, recv_t, end_t, t_send, t_recv)

    send_s[...] = before[-1]
    pl.semaphore_wait(barrier, n_head - 1 + seq_peers)

    s_begin()

    loads[3].wait()
    for b in range(blocks):
        keep(q_in, q_h, q_l, b)
        q_b, k_b = pair(q_h, q_l, b), pair(k_h, k_l, b)
        scores = jnp.where(t_row >= t_col, rows_by_rows(q_b, k_b), 0.0)
        scaled[take(b), :] = times(split(scores), pair(v_h, v_l, b))

    s_relay()
    s_arrive()

    loads[4].wait()
    loads[5].wait()
    scale = head_scale[0]
    gains = gain[...].reshape(1, d)
    for b in range(blocks):
        state = recv_s[...] + before[b]
        mine = (scaled[take(b), :] + times_state(pair(q_h, q_l, b), split(state))) * scale
        scaled[take(b), :] = mine
        square = row_sums(mine * mine)
        cross = row_sums(gains * g_in[take(b), :] * mine)
        for j in range(per):
            sums[b * per + j : b * per + j + 1, :] = square[:, j * GROUP : (j + 1) * GROUP]
            sums[half + b * per + j : half + b * per + j + 1, :] = cross[:, j * GROUP : (j + 1) * GROUP]

    shares = [
        pltpu.make_async_remote_copy(
            src_ref=sums, dst_ref=sums_in.at[step - 1],
            send_sem=h_send.at[step - 1], recv_sem=h_recv.at[step - 1],
            device_id={"head": lax.rem(head + step, n_head)},
            device_id_type=pl.DeviceIdType.MESH,
        )
        for step in range(1, n_head)
    ]
    for share in shares:
        share.start()

    for b in range(blocks):
        q_b, k_b = pair(q_h, q_l, b), pair(k_h, k_l, b)
        scores_t = jnp.where(t_row <= t_col, rows_by_rows(k_b, q_b), 0.0)
        p_h[take(b), :], p_l[take(b), :] = split(scores_t)

    total = sums[...]
    for step in range(1, n_head):
        shares[step - 1].wait_recv()
        total = total + sums_in[step - 1]
    features = d * n_head
    inverse = lax.rsqrt(total[:half] / features + EPS)
    factor = inverse * inverse * inverse * total[half:] / features
    columns = jnp.transpose(jnp.concatenate([inverse, factor], axis=0))

    t_states = []
    for b in range(blocks):
        inv = jnp.concatenate(
            [jnp.broadcast_to(columns[:, b * per + j : b * per + j + 1], (GROUP, d)) for j in range(per)], axis=0
        )
        fac = jnp.concatenate(
            [jnp.broadcast_to(columns[:, half + b * per + j : half + b * per + j + 1], (GROUP, d)) for j in range(per)],
            axis=0,
        )
        mine = scaled[take(b), :]
        weight = inv * gains
        normed[take(b), :] = mine * weight
        grad = (weight * g_in[take(b), :] - mine * fac) * scale
        grad = jnp.where(row + b * block < live, grad, 0.0)
        o_h[take(b), :], o_l[take(b), :] = split(grad)
        t_states.append(outer(pair(q_h, q_l, b), pair(o_h, o_l, b)))
    after = [jnp.zeros((d, d), F32)]
    for b in range(blocks - 1, -1, -1):
        after.append(after[-1] + t_states[b])
    after = after[::-1]

    send_t[...] = after[0]

    t_begin()
    for b in range(blocks):
        o_b, v_b = pair(o_h, o_l, b), pair(v_h, v_l, b)
        pulled = jnp.where(t_row >= t_col, rows_by_rows(o_b, v_b), 0.0)
        pulled_t = jnp.where(t_row <= t_col, rows_by_rows(v_b, o_b), 0.0)
        state = recv_s[...] + before[b]
        gq[take(b), :] = times_state_t(o_b, split(state)) + times(split(pulled), pair(k_h, k_l, b))
        gk[take(b), :] = times(split(pulled_t), pair(q_h, q_l, b))
        gv[take(b), :] = times(pair(p_h, p_l, b), o_b)

    t_relay()
    t_arrive()
    for b in range(blocks):
        t_out[b] = recv_t[...] + after[b + 1]

    for share in shares:
        share.wait_send()

    s_close()
    t_close()


def finish(
    block, normed, gq, gk, gv, k_h, k_l, v_h, v_l, t_in,
    normed_hbm, gq_hbm, gk_hbm, gv_hbm, gk_all, gv_all, sem,
):
    blocks = t_in.shape[0]
    stores = [
        pltpu.make_async_copy(normed, normed_hbm, sem.at[2 * blocks]),
        pltpu.make_async_copy(gq, gq_hbm, sem.at[2 * blocks + 1]),
    ]
    for store in stores:
        store.start()
    for b in range(blocks):
        rows = pl.ds(b * block, block)
        state = split(t_in[b])
        gk_all[rows, :] = gk[rows, :] + times_state_t((v_h[rows, :], v_l[rows, :]), state)
        gv_all[rows, :] = gv[rows, :] + times_state((k_h[rows, :], k_l[rows, :]), state)
        for i, (src, dst) in enumerate(((gk_all, gk_hbm), (gv_all, gv_hbm))):
            store = pltpu.make_async_copy(src.at[rows, :], dst.at[rows, :], sem.at[2 * b + i])
            store.start()
            stores.append(store)
    for store in stores:
        store.wait()


def on_device(n_seq, n_head, query, key_in, value, out_grad, head_scale, norm_gain, group_counts):
    cap, d = query.shape
    block = 2 * GROUP if cap % (2 * GROUP) == 0 else GROUP
    half = -(-(cap // GROUP) // 8) * 8
    blocks = cap // block
    hbm = pl.BlockSpec(memory_space=pltpu.HBM)
    vmem = pl.BlockSpec(memory_space=pltpu.VMEM)
    wide = pltpu.VMEM((cap, d), F32)
    narrow = pltpu.VMEM((cap, d), BF16)
    state = pltpu.VMEM((d, d), F32)
    rows = jax.ShapeDtypeStruct((cap, d), F32)
    rows_low = jax.ShapeDtypeStruct((cap, d), BF16)
    held = pl.pallas_call(
        functools.partial(kernel, n_seq, n_head, block),
        out_shape=[rows] * 4 + [rows_low] * 4 + [jax.ShapeDtypeStruct((blocks, d, d), F32)],
        in_specs=[pl.BlockSpec(memory_space=pltpu.SMEM)] + [hbm] * 6,
        out_specs=[vmem] * 9,
        scratch_shapes=[pltpu.SMEM(group_counts.shape, jnp.int32)]
        + [wide] * 4 + [pltpu.VMEM((d,), F32)]
        + [narrow] * 4 + [pltpu.VMEM((cap, block), BF16)] * 2
        + [wide]
        + [state] * 6
        + [pltpu.VMEM((2 * half, GROUP), F32), pltpu.VMEM((n_head - 1, 2 * half, GROUP), F32)]
        + [pltpu.SemaphoreType.DMA((6,))]
        + [pltpu.SemaphoreType.DMA((CHUNKS,))] * 4
        + [pltpu.SemaphoreType.DMA((n_head - 1,))] * 2
        + [pltpu.SemaphoreType.DMA((2, n_seq)), pltpu.SemaphoreType.DMA((2,))],
        compiler_params=pltpu.CompilerParams(
            collective_id=0, has_side_effects=True, vmem_limit_bytes=32 * 1024 * 1024
        ),
    )(head_scale, *(
        pltpu.with_memory_space_constraint(x, pltpu.HBM)
        for x in (group_counts, query, key_in, value, out_grad, norm_gain)
    ))
    return pl.pallas_call(
        functools.partial(finish, block),
        out_shape=[rows] * 4,
        in_specs=[vmem] * 9,
        out_specs=[hbm] * 4,
        scratch_shapes=[wide] * 2 + [pltpu.SemaphoreType.DMA((2 * blocks + 2,))],
        compiler_params=pltpu.CompilerParams(vmem_limit_bytes=32 * 1024 * 1024),
    )(*held)


def solution(mesh):
    rows = P("seq", "head")
    return jax.shard_map(
        functools.partial(on_device, mesh.shape["seq"], mesh.shape["head"]),
        mesh=mesh,
        in_specs=(rows, rows, rows, rows, P("head"), P("head"), P()),
        out_specs=(rows, rows, rows, rows),
        check_vma=False,
    )
```

```python
import functools

import jax
import jax.numpy as jnp
from jax import lax
from jax.experimental import pallas as pl
from jax.experimental.pallas import tpu as pltpu
from jax.sharding import PartitionSpec as P

GROUP = 128
CHUNKS = 4
EPS = 1e-05
F32 = jnp.float32
BF16 = jnp.bfloat16
NN = (((1,), (0,)), ((), ()))
NT = (((1,), (1,)), ((), ()))
TN = (((0,), (0,)), ((), ()))


def dot(left, right, dims):
    return lax.dot_general(left, right, dims, preferred_element_type=F32)


def split(x):
    high = x.astype(BF16)
    low = (x - high.astype(F32)).astype(BF16)
    return high, low


def rows_by_rows(a, b):
    left = jnp.concatenate([a[0], a[1], a[0]], axis=1)
    right = jnp.concatenate([b[0], b[0], b[1]], axis=1)
    return dot(left, right, NT)


def times(a, b):
    d = b[0].shape[1]
    both = dot(a[0], jnp.concatenate([b[0], b[1]], axis=1), NN)
    return both[:, :d] + both[:, d:] + dot(a[1], b[0], NN)


def times_state(a, s):
    d = s[0].shape[1]
    left = jnp.concatenate([a[0], a[1]], axis=1)
    top = jnp.concatenate([s[0], s[1]], axis=1)
    bottom = jnp.concatenate([s[0], jnp.zeros_like(s[0])], axis=1)
    both = dot(left, jnp.concatenate([top, bottom], axis=0), NN)
    return both[:, :d] + both[:, d:]


def times_state_t(a, s):
    d = s[0].shape[0]
    left = jnp.concatenate([a[0], a[1]], axis=1)
    top = jnp.concatenate([s[0], s[0]], axis=1)
    bottom = jnp.concatenate([s[1], jnp.zeros_like(s[1])], axis=1)
    both = dot(left, jnp.concatenate([top, bottom], axis=0), NT)
    return both[:, :d] + both[:, d:]


def outer(a, b):
    d = a[0].shape[1]
    full = dot(jnp.concatenate(a, axis=1), jnp.concatenate(b, axis=1), TN)
    return full[:d, :d] + full[:d, d:] + full[d:, :d] + full[d:, d:]


def row_sums(x):
    high, low = split(x)
    low2 = (x - high.astype(F32) - low.astype(F32)).astype(BF16)
    parts = jnp.concatenate([high, low, low2], axis=1)
    return dot(jnp.ones((8, parts.shape[1]), BF16), parts, NT)[0:1]


def kernel(
    n_seq, n_head, block, head_scale, counts_hbm,
    q_hbm, k_hbm, v_hbm, g_hbm, gain_hbm,
    normed, gq, gk, gv, k_h, k_l, v_h, v_l, t_out,
    counts, q_in, k_in, v_in, g_in, gain,
    q_h, q_l, o_h, o_l, p_h, p_l,
    scaled, send_s, recv_s, send_t, recv_t, end_s, end_t, sums, sums_in,
    in_sem, s_send, s_recv, t_send, t_recv, h_send, h_recv, e_send, e_recv,
):
    cap, d = q_in.shape
    blocks = cap // block
    per = block // GROUP
    pos = lax.axis_index("seq")
    head = lax.axis_index("head")
    half = sums.shape[0] // 2

    loads = [
        pltpu.make_async_copy(src, dst, in_sem.at[i])
        for i, (src, dst) in enumerate(
            (
                (counts_hbm, counts), (k_hbm, k_in), (v_hbm, v_in), (q_hbm, q_in),
                (g_hbm, g_in), (gain_hbm, gain),
            )
        )
    ]
    for load in loads:
        load.start()

    first, last = pos == 0, pos == n_seq - 1
    barrier = pltpu.get_barrier_semaphore()

    direct = n_seq == 4

    def greet(other):
        pl.semaphore_signal(barrier, inc=1, device_id={"seq": other}, device_id_type=pl.DeviceIdType.MESH)

    seq_peers = 0
    for delta in (-2, -1, 1, 2):
        there = jnp.logical_and(pos + delta >= 0, pos + delta < n_seq)

        @pl.when(there)
        def _():
            greet(pos + delta)

        seq_peers = seq_peers + jnp.where(there, 1, 0)

    for step in range(1, n_head):
        pl.semaphore_signal(
            barrier, inc=1, device_id={"head": lax.rem(head + step, n_head)},
            device_id_type=pl.DeviceIdType.MESH,
        )

    loads[0].wait()
    live = counts[pos] * GROUP
    row = lax.broadcasted_iota(jnp.int32, (block, d), 0)
    t_row = lax.broadcasted_iota(jnp.int32, (block, block), 0)
    t_col = lax.broadcasted_iota(jnp.int32, (block, block), 1)

    def take(b):
        return pl.ds(b * block, block)

    def pair(high, low, b):
        return high[take(b), :], low[take(b), :]

    def keep(source, high, low, b):
        x = jnp.where(row + b * block < live, source[take(b), :], 0.0)
        high[take(b), :], low[take(b), :] = split(x)

    sums[...] = jnp.zeros_like(sums)
    loads[1].wait()
    loads[2].wait()
    states = []
    for b in range(blocks):
        keep(k_in, k_h, k_l, b)
        keep(v_in, v_h, v_l, b)
        states.append(outer(pair(k_h, k_l, b), pair(v_h, v_l, b)))
    before = [jnp.zeros((d, d), F32)]
    for b in range(blocks):
        before.append(before[-1] + states[b])

    def piece(c):
        return pl.ds(c * (d // CHUNKS), d // CHUNKS)

    def hop(src, dst, s_sem, r_sem, c, target):
        return pltpu.make_async_remote_copy(
            src_ref=src.at[piece(c), :], dst_ref=dst.at[piece(c), :],
            send_sem=s_sem.at[c], recv_sem=r_sem.at[c],
            device_id={"seq": target}, device_id_type=pl.DeviceIdType.MESH,
        )

    def far(src, dst, s_sem, r_sem, target):
        return pltpu.make_async_remote_copy(
            src_ref=src, dst_ref=dst, send_sem=s_sem, recv_sem=r_sem,
            device_id={"seq": target}, device_id_type=pl.DeviceIdType.MESH,
        )

    def part(ref, c):
        return ref.at[piece(c), :]

    def exchange(way, src, dst, end, s_sem, r_sem):
        delta = 1 if way == 0 else -1
        order = pos if way == 0 else n_seq - 1 - pos
        first, last = order == 0, order == n_seq - 1

        def neighbour(c):
            return hop(src, dst, s_sem, r_sem, c, pos + delta)

        def skip(c):
            return far(part(src, c), part(dst, c), e_send.at[way, c], r_sem.at[c], pos + 2 * delta)

        def own():
            return far(src, end, e_send.at[way, CHUNKS], e_recv.at[way, CHUNKS], pos + delta)

        def begin():
            @pl.when(first)
            def _():
                for c in range(CHUNKS):
                    neighbour(c).start()
                dst[...] = jnp.zeros_like(dst)

            if direct:

                @pl.when(order == 2)
                def _():
                    own().start()

        def relay():
            @pl.when(jnp.logical_not(first))
            def _():
                for c in range(CHUNKS):
                    neighbour(c).wait_recv()

                    @pl.when(order == 1 if direct else jnp.logical_not(last))
                    def _():
                        src[piece(c), :] += dst[piece(c), :]
                        if direct:
                            skip(c).start()
                        else:
                            neighbour(c).start()

                if direct:

                    @pl.when(order == 1)
                    def _():
                        for c in range(CHUNKS):
                            neighbour(c).start()

            if direct:

                @pl.when(last)
                def _():
                    own().wait_recv()
                    dst[...] += end[...]

        def close():
            @pl.when(order <= 1 if direct else jnp.logical_not(last))
            def _():
                for c in range(CHUNKS):
                    neighbour(c).wait_send()

            if direct:

                @pl.when(order == 1)
                def _():
                    for c in range(CHUNKS):
                        skip(c).wait_send()

                @pl.when(order == 2)
                def _():
                    own().wait_send()

        return begin, relay, close

    s_begin, s_relay, s_close = exchange(0, send_s, recv_s, end_s, s_send, s_recv)
    t_begin, t_relay, t_close = exchange(1, send_t, recv_t, end_t, t_send, t_recv)

    send_s[...] = before[-1]
    pl.semaphore_wait(barrier, n_head - 1 + seq_peers)

    s_begin()

    loads[3].wait()
    for b in range(blocks):
        keep(q_in, q_h, q_l, b)
        q_b, k_b = pair(q_h, q_l, b), pair(k_h, k_l, b)
        scores = jnp.where(t_row >= t_col, rows_by_rows(q_b, k_b), 0.0)
        scaled[take(b), :] = times(split(scores), pair(v_h, v_l, b))

    s_relay()

    loads[4].wait()
    loads[5].wait()
    scale = head_scale[0]
    gains = gain[...].reshape(1, d)
    for b in range(blocks):
        state = recv_s[...] + before[b]
        mine = (scaled[take(b), :] + times_state(pair(q_h, q_l, b), split(state))) * scale
        scaled[take(b), :] = mine
        square = row_sums(mine * mine)
        cross = row_sums(gains * g_in[take(b), :] * mine)
        for j in range(per):
            sums[b * per + j : b * per + j + 1, :] = square[:, j * GROUP : (j + 1) * GROUP]
            sums[half + b * per + j : half + b * per + j + 1, :] = cross[:, j * GROUP : (j + 1) * GROUP]

    shares = [
        pltpu.make_async_remote_copy(
            src_ref=sums, dst_ref=sums_in.at[step - 1],
            send_sem=h_send.at[step - 1], recv_sem=h_recv.at[step - 1],
            device_id={"head": lax.rem(head + step, n_head)},
            device_id_type=pl.DeviceIdType.MESH,
        )
        for step in range(1, n_head)
    ]
    for share in shares:
        share.start()

    for b in range(blocks):
        q_b, k_b = pair(q_h, q_l, b), pair(k_h, k_l, b)
        scores_t = jnp.where(t_row <= t_col, rows_by_rows(k_b, q_b), 0.0)
        p_h[take(b), :], p_l[take(b), :] = split(scores_t)

    total = sums[...]
    for step in range(1, n_head):
        shares[step - 1].wait_recv()
        total = total + sums_in[step - 1]
    features = d * n_head
    inverse = lax.rsqrt(total[:half] / features + EPS)
    factor = inverse * inverse * inverse * total[half:] / features
    columns = jnp.transpose(jnp.concatenate([inverse, factor], axis=0))

    t_states = []
    for b in range(blocks):
        inv = jnp.concatenate(
            [jnp.broadcast_to(columns[:, b * per + j : b * per + j + 1], (GROUP, d)) for j in range(per)], axis=0
        )
        fac = jnp.concatenate(
            [jnp.broadcast_to(columns[:, half + b * per + j : half + b * per + j + 1], (GROUP, d)) for j in range(per)],
            axis=0,
        )
        mine = scaled[take(b), :]
        weight = inv * gains
        normed[take(b), :] = mine * weight
        grad = (weight * g_in[take(b), :] - mine * fac) * scale
        grad = jnp.where(row + b * block < live, grad, 0.0)
        o_h[take(b), :], o_l[take(b), :] = split(grad)
        t_states.append(outer(pair(q_h, q_l, b), pair(o_h, o_l, b)))
    after = [jnp.zeros((d, d), F32)]
    for b in range(blocks - 1, -1, -1):
        after.append(after[-1] + t_states[b])
    after = after[::-1]

    send_t[...] = after[0]

    t_begin()
    for b in range(blocks):
        o_b, v_b = pair(o_h, o_l, b), pair(v_h, v_l, b)
        pulled = jnp.where(t_row >= t_col, rows_by_rows(o_b, v_b), 0.0)
        pulled_t = jnp.where(t_row <= t_col, rows_by_rows(v_b, o_b), 0.0)
        state = recv_s[...] + before[b]
        gq[take(b), :] = times_state_t(o_b, split(state)) + times(split(pulled), pair(k_h, k_l, b))
        gk[take(b), :] = times(split(pulled_t), pair(q_h, q_l, b))
        gv[take(b), :] = times(pair(p_h, p_l, b), o_b)

    t_relay()
    for b in range(blocks):
        t_out[b] = recv_t[...] + after[b + 1]

    for share in shares:
        share.wait_send()

    s_close()
    t_close()


def finish(
    block, normed, gq, gk, gv, k_h, k_l, v_h, v_l, t_in,
    normed_hbm, gq_hbm, gk_hbm, gv_hbm, gk_all, gv_all, sem,
):
    blocks = t_in.shape[0]
    stores = [
        pltpu.make_async_copy(normed, normed_hbm, sem.at[2 * blocks]),
        pltpu.make_async_copy(gq, gq_hbm, sem.at[2 * blocks + 1]),
    ]
    for store in stores:
        store.start()
    for b in range(blocks):
        rows = pl.ds(b * block, block)
        state = split(t_in[b])
        gk_all[rows, :] = gk[rows, :] + times_state_t((v_h[rows, :], v_l[rows, :]), state)
        gv_all[rows, :] = gv[rows, :] + times_state((k_h[rows, :], k_l[rows, :]), state)
        for i, (src, dst) in enumerate(((gk_all, gk_hbm), (gv_all, gv_hbm))):
            store = pltpu.make_async_copy(src.at[rows, :], dst.at[rows, :], sem.at[2 * b + i])
            store.start()
            stores.append(store)
    for store in stores:
        store.wait()


def on_device(n_seq, n_head, query, key_in, value, out_grad, head_scale, norm_gain, group_counts):
    cap, d = query.shape
    block = 2 * GROUP if cap % (2 * GROUP) == 0 else GROUP
    half = -(-(cap // GROUP) // 8) * 8
    blocks = cap // block
    hbm = pl.BlockSpec(memory_space=pltpu.HBM)
    vmem = pl.BlockSpec(memory_space=pltpu.VMEM)
    wide = pltpu.VMEM((cap, d), F32)
    narrow = pltpu.VMEM((cap, d), BF16)
    state = pltpu.VMEM((d, d), F32)
    rows = jax.ShapeDtypeStruct((cap, d), F32)
    rows_low = jax.ShapeDtypeStruct((cap, d), BF16)
    held = pl.pallas_call(
        functools.partial(kernel, n_seq, n_head, block),
        out_shape=[rows] * 4 + [rows_low] * 4 + [jax.ShapeDtypeStruct((blocks, d, d), F32)],
        in_specs=[pl.BlockSpec(memory_space=pltpu.SMEM)] + [hbm] * 6,
        out_specs=[vmem] * 9,
        scratch_shapes=[pltpu.SMEM(group_counts.shape, jnp.int32)]
        + [wide] * 4 + [pltpu.VMEM((d,), F32)]
        + [narrow] * 4 + [pltpu.VMEM((cap, block), BF16)] * 2
        + [wide]
        + [state] * 6
        + [pltpu.VMEM((2 * half, GROUP), F32), pltpu.VMEM((n_head - 1, 2 * half, GROUP), F32)]
        + [pltpu.SemaphoreType.DMA((6,))]
        + [pltpu.SemaphoreType.DMA((CHUNKS,))] * 4
        + [pltpu.SemaphoreType.DMA((n_head - 1,))] * 2
        + [pltpu.SemaphoreType.DMA((2, CHUNKS + 1)), pltpu.SemaphoreType.DMA((2, CHUNKS + 1))],
        compiler_params=pltpu.CompilerParams(
            collective_id=0, has_side_effects=True, vmem_limit_bytes=32 * 1024 * 1024
        ),
    )(head_scale, *(
        pltpu.with_memory_space_constraint(x, pltpu.HBM)
        for x in (group_counts, query, key_in, value, out_grad, norm_gain)
    ))
    return pl.pallas_call(
        functools.partial(finish, block),
        out_shape=[rows] * 4,
        in_specs=[vmem] * 9,
        out_specs=[hbm] * 4,
        scratch_shapes=[wide] * 2 + [pltpu.SemaphoreType.DMA((2 * blocks + 2,))],
        compiler_params=pltpu.CompilerParams(vmem_limit_bytes=32 * 1024 * 1024),
    )(*held)


def solution(mesh):
    rows = P("seq", "head")
    return jax.shard_map(
        functools.partial(on_device, mesh.shape["seq"], mesh.shape["head"]),
        mesh=mesh,
        in_specs=(rows, rows, rows, rows, P("head"), P("head"), P()),
        out_specs=(rows, rows, rows, rows),
        check_vma=False,
    )
```
